32 devices in a mesh: wide: 16 (over z, y, x), narrow: 2 (over core).
Axes of the slice: x: 2, y: 2, z: 4, core: 2. Of those that a mesh axis runs over, the one named last changes fastest.
Arguments:
- queries: bfloat16 [4096, 768], P(('wide', 'narrow')), may hold values from -40 to 40
- table: bfloat16 [2048, 768], P('wide'), may hold values from -6 to 6
- head: bfloat16 [768, 768], replicated, may hold values from -0.21875 to 0.21875
- pos_ids: int32 [4096], P(('wide', 'narrow')), may hold values from 0 to 2047, as said below
- neg_ids: int32 [4096, 8], P(('wide', 'narrow')), may hold values from 0 to 2047, as said below
- loss_weights: float32 [4096], P(('wide', 'narrow')), may hold values from 8 to 64
Outputs:
- d_queries: float32 [4096, 768], P(('wide', 'narrow'))
- d_table: float32 [2048, 768], P(('wide', 'narrow'))
- d_head: float32 [768, 768], replicated
The draws below stay inside these ranges and needn't reach their ends.
Inputs may be any that keep to these rules, and one draw needn't show every extreme that they name: `pos_ids`: the queries form aligned blocks of 128 (the queries of one device). Within a block at most 16 positives lie in one shard of 128 consecutive passage rows (shard = id // 128); one shard, the same for every block, holds exactly 16 of every block. `neg_ids`: within each aligned block of 128 queries, at most 96 of its 1024 negatives lie in one shard of 128 consecutive passage rows (shard = id // 128); one shard, the same for every block, holds exactly 96 of every block. Popular rows recur.
All inputs are finite; a program needn't handle non-finite values.
Results may differ from the reference program's by a relative error of at most 0.0063.
Values may be sent and summed in bfloat16 or wider, within the bound.
A program may use at most 64 MiB of HBM per device.

```python
import math
from functools import partial
import jax
import jax.numpy as jnp
from jax import lax

D = 768
NEG = 8
QRY_DEV = 128
ROWS_DEV = 128
POS_CAP = 16
NEG_CAP = 96
QUERIES = 4096
PASSAGES = 2048
N_WIDE = 16
N_NARROW = 2


def make_table(key):
    base = jax.random.fold_in(key, 11)
    values = jnp.clip(jax.random.normal(base, (PASSAGES, D), jnp.float32), -6.0, 6.0)
    return values


def spread_owners(block_key, count_slots, capacity, hottest):
    remain = count_slots - capacity
    lowest = max(1, -(-remain // (N_WIDE - 1)))
    len_key, order_key, mix_key = jax.random.split(block_key, 3)
    run_lengths = jax.random.randint(len_key, (N_WIDE - 1,), lowest, capacity + 1)
    others = jnp.arange(N_WIDE - 1, dtype=jnp.int32)
    others = others + (others >= hottest).astype(jnp.int32)
    others = jax.random.permutation(order_key, others)
    bounds = jnp.cumsum(run_lengths)
    positions = jnp.arange(remain, dtype=jnp.int32)
    bucket_of = jnp.sum((bounds[None, :] <= positions[:, None]).astype(jnp.int32), axis=1)
    owners = jnp.concatenate([jnp.full((capacity,), hottest, jnp.int32), others[bucket_of]])
    return jax.random.permutation(mix_key, owners)


def make_ids(key, per_query, capacity, salt):
    base = jax.random.fold_in(jax.random.fold_in(key, 23), salt)
    hot_key, pop_key, block_key, local_key = jax.random.split(base, 4)
    hottest = jax.random.randint(hot_key, (), 0, N_WIDE)
    blocks = N_WIDE * N_NARROW
    per_block = QRY_DEV * per_query
    spreader = partial(spread_owners, count_slots=per_block, capacity=capacity, hottest=hottest)
    owners = jax.vmap(spreader)(jax.random.split(block_key, blocks))
    picks = jax.random.randint(local_key, (blocks, per_block, 2), 0, ROWS_DEV)
    skewed = picks[:, :, 0] * picks[:, :, 1] // ROWS_DEV
    popular = jax.random.permutation(pop_key, jnp.arange(ROWS_DEV, dtype=jnp.int32))
    return (owners * ROWS_DEV + popular[skewed]).reshape(QUERIES, per_query)


def draw_pos_ids(key, part):
    return make_ids(key, 1, POS_CAP, 1).reshape(QUERIES)


def draw_neg_ids(key, part):
    return make_ids(key, NEG, NEG_CAP, 2)


def draw_table(key, part):
    return make_table(key).astype(jnp.bfloat16)


def draw_queries(key, part):
    table = make_table(key)
    positive = draw_pos_ids(key, part)
    negative = draw_neg_ids(key, part)
    noise = jax.random.normal(jax.random.fold_in(key, 31), (QUERIES, D), jnp.float32)
    noise = jnp.clip(noise, -6.0, 6.0)
    hard_sum = jnp.zeros((QUERIES, D), jnp.float32)
    for column in range(NEG):
        hard_sum = hard_sum + table[negative[:, column]]
    mixed = 0.8 * noise + 0.15 * table[positive] + 0.13 * hard_sum
    return mixed.astype(jnp.bfloat16)


def steps_of(rng, shape, pieces, least, largest):
    def one(dim, parts):
        steps = jax.random.uniform(jax.random.fold_in(jax.random.fold_in(rng, 6), dim), (parts,), jnp.float32, least / len(pieces), largest / len(pieces))
        return jnp.repeat(jnp.exp(steps), shape[dim] // parts).reshape((-1,) + (1,) * (len(shape) - dim - 1))

    loudness = one(*pieces[0])
    for cut in pieces[1:]:
        loudness = loudness * one(*cut)
    return loudness


def normal_values(stream_key, extent, width, most, kind=jnp.bfloat16):
    entries = jax.random.normal(stream_key, extent, jnp.float32) * width
    return jnp.minimum(jnp.maximum(entries, -most), most).astype(kind)


def setup_inputs(seed: int = 0) -> dict:
    splits = jax.random.split(jax.random.key(seed), 7)
    return {
        "queries": draw_queries(jax.random.fold_in(splits[6], 71), 0),
        "table": draw_table(jax.random.fold_in(splits[6], 71), 0),
        "head": normal_values(splits[2], (D, D), D ** -0.5, 0.21875),
        "pos_ids": draw_pos_ids(jax.random.fold_in(splits[6], 71), 0),
        "neg_ids": draw_neg_ids(jax.random.fold_in(splits[6], 71), 0),
        "loss_weights": jnp.clip(jnp.exp(math.log(64.0) - 2.0794415 * jax.random.uniform(splits[5], (QUERIES,), jnp.float32) ** steps_of(splits[5], (QUERIES,), ((0, 32),), -0.2, 0.2)), 8.0, 64.0),
    }


def reference(queries, table, head, pos_ids, neg_ids, loss_weights):
    scale = float(D) ** -0.5
    group = N_NARROW * QRY_DEV
    query_proj = jnp.dot(queries, head, preferred_element_type=jnp.float32).astype(jnp.bfloat16)
    table_proj = jnp.dot(table, head, preferred_element_type=jnp.float32).astype(jnp.bfloat16)
    positions = jnp.arange(group, dtype=jnp.int32)
    target = (positions[:, None] == positions[None, :]).astype(jnp.float32)

    def one_group(row_total, index):
        start = (index * group).astype(jnp.int32)
        query_block = lax.dynamic_slice_in_dim(query_proj, start, group, 0)
        pos_block = lax.dynamic_slice_in_dim(pos_ids, start, group, 0)
        neg_block = lax.dynamic_slice_in_dim(neg_ids, start, group, 0)
        weight_block = lax.dynamic_slice_in_dim(loss_weights, start, group, 0)
        keys = jnp.take(table_proj, pos_block, axis=0)
        negatives = jnp.take(table_proj, neg_block, axis=0)
        in_scores = jnp.dot(query_block, keys.T, preferred_element_type=jnp.float32) * scale
        neg_scores = jnp.einsum("bd,bnd->bn", query_block.astype(jnp.float32), negatives.astype(jnp.float32), precision=lax.Precision.HIGHEST) * scale
        top = jnp.maximum(jnp.max(in_scores, axis=1), jnp.max(neg_scores, axis=1))
        total = jnp.sum(jnp.exp(in_scores - top[:, None]), axis=1) + jnp.sum(jnp.exp(neg_scores - top[:, None]), axis=1)
        log_total = top + jnp.log(total)
        in_probs = jnp.exp(in_scores - log_total[:, None])
        neg_probs = jnp.exp(neg_scores - log_total[:, None])
        in_coef = (weight_block[:, None] * (in_probs - target) * scale).astype(jnp.bfloat16)
        neg_coef = (weight_block[:, None] * neg_probs * scale).astype(jnp.bfloat16)
        grad_query = jnp.dot(in_coef, keys, preferred_element_type=jnp.float32)
        grad_query = grad_query + jnp.einsum("bn,bnd->bd", neg_coef.astype(jnp.float32), negatives.astype(jnp.float32), precision=lax.Precision.HIGHEST)
        key_grad = jnp.dot(in_coef.T, query_block, preferred_element_type=jnp.float32)
        neg_grad = neg_coef.astype(jnp.float32)[:, :, None] * query_block.astype(jnp.float32)[:, None, :]
        row_total = row_total.at[pos_block].add(key_grad)
        row_total = row_total.at[neg_block.reshape(-1)].add(neg_grad.reshape(-1, D))
        return row_total, grad_query.astype(jnp.bfloat16)

    row_total, grad_blocks = lax.scan(one_group, jnp.zeros((PASSAGES, D), jnp.float32), jnp.arange(N_WIDE, dtype=jnp.int32))
    grad_query = grad_blocks.reshape(QUERIES, D)
    d_queries = jnp.dot(grad_query, head.T, preferred_element_type=jnp.float32)
    row_grad = row_total.astype(jnp.bfloat16)
    d_table = jnp.dot(row_grad, head.T, preferred_element_type=jnp.float32)
    d_head = jnp.dot(queries.T, grad_query, preferred_element_type=jnp.float32) + jnp.dot(table.T, row_grad, preferred_element_type=jnp.float32)
    return d_queries, d_table, d_head
```

```python
import functools
import math

import jax
import jax.numpy as jnp
from jax import lax
from jax.experimental import pallas as pl
from jax.experimental.pallas import tpu as pltpu
from jax.sharding import PartitionSpec as P

BOTH = ("wide", "narrow")
MESH = pl.DeviceIdType.MESH
NT = (((1,), (1,)), ((), ()))
TN = (((0,), (0,)), ((), ()))
F32 = jnp.float32
BF16 = jnp.bfloat16
LOW = -1e30


def dot(a, b, dims=(((1,), (0,)), ((), ()))):
    return lax.dot_general(a, b, dims, preferred_element_type=F32)


class Net:
    def __init__(self, wide, narrow, send_sem, recv_sem):
        self.wide, self.narrow, self.depth = wide, narrow, wide // 4
        self.send_sem, self.recv_sem = send_sem, recv_sem
        self.w = lax.axis_index("wide")
        self.n = lax.axis_index("narrow")
        self.z = self.w // 4
        y, x = (self.w // 2) % 2, self.w % 2
        self.x, self.y = x, y
        self.px = (self.w + 1 - 2 * x, self.n)
        self.py = (self.w + 2 - 4 * y, self.n)
        self.pd = (self.w + 3 - 2 * x - 4 * y, self.n)
        self.me = y * 2 + x
        xn, yn = y * 2 + 1 - x, (1 - y) * 2 + x
        self.chips = (self.me, xn, yn, (1 - y) * 2 + 1 - x)
        self.used = 0
        self.started, self.guarded = [], []

    def owner(self, j, e):
        return lax.rem(self.z + e, self.depth) * 4 + self.chips[j]

    def zpeer(self, d):
        return (self.owner(0, d), self.n)

    def sibling(self, d):
        return (self.w, lax.rem(self.n + d, self.narrow))

    def mate(self, c, d):
        return (self.px[0] if c else self.w, lax.rem(self.n + d, self.narrow))

    def place(self, c, d):
        x = 1 - self.x if c else self.x
        return x * self.narrow + lax.rem(self.n - d + self.narrow, self.narrow)

    def mates(self):
        return [(c, d) for c in range(2) for d in range(self.narrow) if c or d]

    def sems(self, count):
        first = self.used
        self.used += count
        return first

    def copy(self, src, dst, sem, device, sent=None):
        return pltpu.make_async_remote_copy(
            src_ref=src,
            dst_ref=dst,
            send_sem=self.send_sem.at[sem if sent is None else sent],
            recv_sem=self.recv_sem.at[sem],
            device_id=device,
            device_id_type=MESH,
        )

    def send(self, src, dst, sem, device):
        copy = self.copy(src, dst, sem, device)
        copy.start()
        self.started.append(copy)

    def arrive(self, dst, sem):
        self.copy(dst, dst, sem, self.px).wait_recv()

    def send_if(self, cond, copy):
        pl.when(cond)(copy.start)
        self.guarded.append((cond, copy))

    def drain(self):
        for copy in self.started:
            copy.wait_send()
        for cond, copy in self.guarded:
            pl.when(cond)(copy.wait_send)
        self.started, self.guarded = [], []

    def peers(self):
        peers = [self.py, self.pd] + [self.zpeer(d) for d in range(1, self.depth)]
        return peers + [self.mate(c, d) for c, d in self.mates()]

    def greet(self):
        sem = pltpu.get_barrier_semaphore()
        for peer in self.peers():
            pl.semaphore_signal(sem, inc=1, device_id=peer, device_id_type=MESH)

    def await_greetings(self):
        pl.semaphore_wait(pltpu.get_barrier_semaphore(), len(self.peers()))


class Gather:
    def __init__(self, net, block):
        self.net, self.block = net, block
        depth = net.depth
        self.zs, self.plane_sem = net.sems(depth), net.sems(4 * depth)

    def to_plane(self, e):
        net, own = self.net, self.block(0, e)
        for j, peer in ((3, net.pd), (1, net.px), (2, net.py)):
            net.send(own, own, self.plane_sem + 4 * e + j, peer)

    def start(self):
        net, own = self.net, self.block(0, 0)
        for d in range(1, net.depth):
            net.send(own, own, self.zs + net.depth - d, net.zpeer(d))
        self.to_plane(0)

    def column(self, e):
        self.net.arrive(self.block(0, e), self.zs + e)
        self.to_plane(e)

    def plane(self, j, e):
        self.net.arrive(self.block(j, e), self.plane_sem + 4 * e + j)


class ColumnGather:
    def __init__(self, net, buf, cuts):
        self.net, self.buf, self.cuts = net, buf, cuts
        count = len(cuts) * net.depth
        self.zs, self.ys, self.fs = net.sems(count), net.sems(count), net.sems(len(cuts))
        self.relay = net.depth == 4

    def pieces(self, j, e):
        for i, cut in enumerate(self.cuts):
            yield e * len(self.cuts) + i, self.buf.at[j, e, :, cut]

    def start(self):
        net, depth = self.net, self.net.depth
        for d in (2, 1, 3) if self.relay else range(1, depth):
            for (_, own), (i, to) in zip(self.pieces(0, 0), self.pieces(0, depth - d)):
                copy = net.copy(own, to, self.zs + i, net.zpeer(d))
                if self.relay and d != 2:
                    net.send_if(net.z != (3 if d == 1 else 0), copy)
                else:
                    copy.start()
                    net.started.append(copy)
        for (i, own), (_, to) in zip(self.pieces(0, 0), self.pieces(1, 0)):
            net.send(own, to, self.ys + i, net.py)

    def column(self, e):
        net, passed = self.net, self.relay and e == 2
        if self.relay:
            e = jnp.where(net.z < 2, e, 4 - e) if e != 2 else e
        end = jnp.where(net.z == 2, 1, 3)
        ends = list(self.pieces(0, end))
        for k, ((i, ref), (_, to)) in enumerate(zip(self.pieces(0, e), self.pieces(1, e))):
            net.arrive(ref, self.zs + i)
            if passed:
                inner = (net.z == 1) | (net.z == 2)
                sem = self.zs + ends[k][0]
                net.send_if(inner, net.copy(ref, ends[k][1], sem, net.zpeer(end), self.fs + k))
            net.send(ref, to, self.ys + i, net.py)

    def plane(self, e):
        for i, ref in self.pieces(1, e):
            self.net.arrive(ref, self.ys + i)


class ColumnScatter:
    def __init__(self, net, value, ref, bufs):
        self.net, self.value, self.ref = net, value, ref
        self.ry, self.zs, self.rz = bufs
        self.ys, self.z = net.sems(net.depth), net.sems(net.depth)

    def first(self, d):
        self.net.send(self.ref.at[d, 1], self.ry.at[d], self.ys + d, self.net.py)

    def second(self, d):
        net = self.net
        net.arrive(self.ry.at[d], self.ys + d)
        total = self.value[d, 0] + self.ry[d].astype(F32)
        if d == 0:
            self.value[0, 0] = total
        else:
            self.zs[d - 1] = total.astype(BF16)
            net.send(self.zs.at[d - 1], self.rz.at[d - 1], self.z + d, net.zpeer(d))

    def last(self):
        total = self.value[0, 0]
        for d in range(1, self.net.depth):
            self.net.arrive(self.rz.at[d - 1], self.z + d)
            total = total + self.rz[d - 1].astype(F32)
        return total


class Scatter:
    def __init__(self, net, value, ref, bufs, half):
        self.net, self.value, self.ref = net, value, ref
        self.ra, self.rb, self.st, self.zs, self.rz, self.total = bufs
        self.halves = (slice(0, half), slice(half, 2 * half))
        self.cuts = (pl.ds(0, half), pl.ds(half, half))
        depth = net.depth
        self.one, self.two, self.z = net.sems(4 * depth), net.sems(2 * depth), net.sems(depth)

    def first(self, order):
        net = self.net
        for slot, blocks in enumerate(((3, 3), (1, 2))):
            for d in order:
                for h, peer in ((0, net.px), (1, net.py)):
                    src = self.ref(blocks[h], d).at[:, self.cuts[h]]
                    sem = self.one + 4 * d + 2 * slot + h
                    net.send(src, self.ra.at[h, slot, d], sem, peer)

    def second(self, d):
        net = self.net
        for h, j, peer in ((0, 2, net.py), (1, 1, net.px)):
            net.arrive(self.ra.at[h, 0, d], self.one + 4 * d + h)
            total = self.value(j, d)[:, self.halves[h]] + self.ra[h, 0, d].astype(F32)
            self.st[h, d] = total.astype(BF16)
            net.send(self.st.at[h, d], self.rb.at[h, d], self.two + 2 * d + h, peer)

    def third(self, d):
        net = self.net
        own = self.value(0, d)
        for h in range(2):
            net.arrive(self.ra.at[h, 1, d], self.one + 4 * d + 2 + h)
            net.arrive(self.rb.at[h, d], self.two + 2 * d + h)
            total = own[:, self.halves[h]] + self.ra[h, 1, d].astype(F32)
            total = total + self.rb[h, d].astype(F32)
            if d == 0:
                self.total[:, self.halves[h]] = total
            else:
                self.zs[d - 1, :, self.halves[h]] = total.astype(BF16)
        if d:
            net.send(self.zs.at[d - 1], self.rz.at[d - 1], self.z + d, net.zpeer(d))

    def last(self):
        total = self.total[...]
        for d in range(1, self.net.depth):
            self.net.arrive(self.rz.at[d - 1], self.z + d)
            total = total + self.rz[d - 1].astype(F32)
        return total


def scatter_bufs(depth, height, width):
    half = width // 2
    return [
        pltpu.VMEM((2, 2, depth, height, half), BF16),
        pltpu.VMEM((2, depth, height, half), BF16),
        pltpu.VMEM((2, depth, height, half), BF16),
        pltpu.VMEM((max(depth - 1, 1), height, width), BF16),
        pltpu.VMEM((max(depth - 1, 1), height, width), BF16),
        pltpu.VMEM((height, width), F32),
    ]


def kernel(
    wide, narrow, reduce_head,
    queries, table, head_in, neg_in, pos_in, weight_in,
    d_queries, d_table, d_head,
    send_sem, recv_sem, load_sem,
    head, query, neg, pos, weight,
    tab, qp, u, count, scores, coef, stats, g_own, g_part, b_part, g_ref, gq, gq_mate,
    p_val, p_ref, p_ry, p_zs, p_rz, *h_bufs,
):
    net = Net(wide, narrow, send_sem, recv_sem)
    depth, n = net.depth, net.n
    batch, width = queries.shape
    half = width // 2
    part = tab.shape[2]
    shard = part * narrow
    span = depth * part
    team = 2 * narrow
    group = team * batch
    negatives = neg_in.shape[0]
    scale = float(width) ** (-0.5)
    me = net.x * narrow + n

    net.greet()
    rows = pl.ds(pl.multiple_of(n * part, part), part)
    loads = [
        pltpu.make_async_copy(table.at[rows, :], tab.at[0, 0], load_sem.at[0]),
        pltpu.make_async_copy(queries, query.at[me], load_sem.at[1]),
        pltpu.make_async_copy(head_in, head, load_sem.at[2]),
        pltpu.make_async_copy(neg_in, neg.at[me], load_sem.at[3]),
        pltpu.make_async_copy(pos_in, pos.at[me], load_sem.at[4]),
        pltpu.make_async_copy(weight_in, weight.at[me], load_sem.at[5]),
    ]
    for load in loads:
        load.start()
    for i in (0, 1, 3, 4, 5):
        loads[i].wait()
    net.await_greetings()

    gather = ColumnGather(net, tab, [pl.ds(i * (width // 3), width // 3) for i in range(3)])
    gather.start()

    def swap(buf):
        first = net.sems(narrow)
        for d in range(1, narrow):
            net.send(buf.at[0], buf.at[d], first + d, net.sibling(d))
        return [(buf.at[d], first + d) for d in range(1, narrow)]

    def spread(buf):
        first = net.sems(team)
        for c, d in net.mates():
            net.send(buf.at[me], buf.at[me], first + c * narrow + d, net.mate(c, d))
        return [(buf.at[net.place(c, d)], first + c * narrow + d) for c, d in net.mates()]

    def arrived(copies):
        for ref, sem in copies:
            net.arrive(ref, sem)

    query_sem = net.sems(team)
    net.send(query.at[me], query.at[me], query_sem + narrow, net.px)
    for d in range(1, narrow):
        net.send(query.at[me], query.at[me], query_sem + d, net.sibling(d))
    small = spread(neg) + spread(pos) + spread(weight)
    for e in range(1, depth):
        gather.column(e)
    across = net.place(1, 0)
    net.arrive(query.at[across], query_sem + narrow)
    for d in range(1, narrow):
        net.send(query.at[across], query.at[across], query_sem + narrow + d, net.sibling(d))
    for c, d in net.mates():
        if d:
            net.arrive(query.at[net.place(c, d)], query_sem + c * narrow + d)
    loads[2].wait()
    arrived(small)

    def lanes(ref):
        return jnp.concatenate([ref[d] for d in range(team)], axis=1)

    def slots(ids):
        chip, local = ids // shard, ids % shard
        block = ((chip // 2) % 2) ^ net.y
        plane = lax.rem(chip // 4 - net.z + depth, depth)
        slot = (block * depth + plane) * part + local % part
        here = (local // part == n) & (chip % 2 == net.x)
        return jnp.where(here, slot, -1)

    negs = slots(lanes(neg))
    own_row = slots(lanes(pos))
    w_row = lanes(weight) * scale

    def own_mask(j):
        row = j * span + lax.broadcasted_iota(jnp.int32, (span, group), 0)
        return row, (own_row == row).astype(F32)

    for j in range(2):
        row, own = own_mask(j)
        for c in range(2):
            half_own = own[:, c * group // 2 : (c + 1) * group // 2]
            keys = jnp.sum(half_own, axis=1, keepdims=True)
            count[j, :, c * group // 2 : (c + 1) * group // 2] = keys + jnp.zeros_like(half_own)
        total = count[j]
        for k in range(negatives):
            total = total + (negs[k : k + 1, :] == row).astype(F32)
        count[j] = total

    qp[...] = dot(query[...].reshape(group, width), head[...]).astype(BF16)
    u[...] = dot(qp[...], head[...], NT).astype(BF16)

    def score(j, top):
        value = dot(tab[j].reshape(span, width), u[...], NT) * scale
        value = jnp.where(count[j] > 0, value, LOW)
        scores[j] = value
        return jnp.maximum(top, jnp.max(value, axis=0, keepdims=True))

    top = score(0, jnp.full((1, group), LOW, F32))

    def own_rows(j):
        _, own = own_mask(j)
        return dot(own.astype(BF16), tab[j].reshape(span, width), TN)

    if reduce_head:
        g_own[...] = own_rows(0)
    for e in range(depth):
        gather.plane(e)
    if reduce_head:
        b_part[0] = (g_own[...] + own_rows(1)).astype(BF16)
        b_copies = swap(b_part)
    top = score(1, top)
    total = jnp.zeros((1, group), F32)
    own_exp = jnp.zeros((1, group), F32)
    for j in range(2):
        _, own = own_mask(j)
        exps = jnp.exp(scores[j] - top)
        value = count[j] * exps
        scores[j] = value
        total = total + jnp.sum(value, axis=0, keepdims=True)
        if reduce_head:
            own_value = own * exps
            own_exp = own_exp + jnp.sum(own_value, axis=0, keepdims=True)
            coef[j] = (value - own_value).astype(BF16).reshape(depth, part, group)
    stats[me, 0:1, :] = top
    stats[me, 1:2, :] = total
    stats[me, 2:3, :] = own_exp
    stats_copies = spread(stats)
    if reduce_head:
        g = dot(coef[0].reshape(span, group), tab[0].reshape(span, width), TN)
        g = g + dot(coef[1].reshape(span, group), tab[1].reshape(span, width), TN)
        g_own[...] = g
        g_part[0] = g.astype(BF16)
        g_copies = swap(g_part)
    arrived(stats_copies)
    best = jnp.max(stats[:, 0:1, :], axis=0)
    factors = jnp.exp(stats[:, 0:1, :] - best)
    everything = jnp.sum(stats[:, 1:2, :] * factors, axis=0)
    own_prob = jnp.sum(stats[:, 2:3, :] * factors, axis=0) / everything
    factor = jnp.exp(top - best) / everything
    for j in range(2):
        _, own = own_mask(j)
        value = w_row * (scores[j] * factor - own)
        coef[j] = value.astype(BF16).reshape(depth, part, group)

    rows_sum = ColumnScatter(net, p_val, p_ref, (p_ry, p_zs, p_rz))

    def row_grads(d):
        piece = jnp.concatenate([coef[0, d], coef[1, d]], axis=0)
        value = dot(piece, u[...]).reshape(2, part, width)
        p_val[d] = value
        p_ref[d] = value.astype(BF16)

    order = sorted(range(1, depth), key=lambda d: -min(d, depth - d)) + [0]

    def queries_of(m):
        return pl.ds(pl.multiple_of(m * batch, batch), batch)

    row_grads(order[0])
    rows_sum.first(order[0])
    if not reduce_head:
        g = dot(coef[0].reshape(span, group), tab[0].reshape(span, width), TN)
        g_own[...] = g + dot(coef[1].reshape(span, group), tab[1].reshape(span, width), TN)
        g_part[...] = g_own[...].astype(BF16).reshape(team, batch, width)
        first = net.sems(team)
        copies = []
        for c, d in net.mates():
            to = (1 - net.x if c else net.x) * narrow + lax.rem(n + d, narrow)
            ref = gq_mate.at[c * narrow + d]
            net.send(g_part.at[to], ref, first + c * narrow + d, net.mate(c, d))
            copies.append((ref, first + c * narrow + d))
        arrived(copies)
        g = g_own[queries_of(me), :]
        for c, d in net.mates():
            g = g + gq_mate[c * narrow + d].astype(F32)
        g = g.astype(BF16)
        grad = dot(g, head[...]).astype(BF16)
        d_queries[...] = dot(grad, head[...], NT)
        d_head[...] = dot(query[me], grad, TN) + dot(g, qp[queries_of(me), :], TN)
        for i in range(depth):
            if i:
                row_grads(order[i])
                rows_sum.first(order[i])
            rows_sum.second(order[i])
        d_table[...] = rows_sum.last()
        net.drain()
        return

    scales = [w_row * (own_prob - 1.0), w_row * factor]
    for d in range(1, narrow):
        theirs = net.place(0, d)
        scales.append(w_row * jnp.exp(stats[theirs, 0:1, :] - best) / everything)
    scales += [jnp.zeros((1, group), F32)] * (-len(scales) % 8)
    scales = jnp.concatenate(scales, axis=0).T
    arrived(g_copies + b_copies)
    rows = b_part[0].astype(F32)
    g = scales[:, 1:2] * g_own[...]
    for d in range(1, narrow):
        rows = rows + b_part[d].astype(F32)
        g = g + scales[:, d + 1 : d + 2] * g_part[d].astype(F32)
    g_ref[...] = (g + scales[:, 0:1] * rows).astype(BF16)
    gq[...] = dot(g_ref[...], head[...]).astype(BF16)

    h_val, h_ref, h_all = h_bufs[:3]
    height = width // (narrow * wide)
    mine = pl.ds(pl.multiple_of(n * (width // narrow), 128), width // narrow)
    for c in range(2):
        cut = slice(c * half, (c + 1) * half)
        value = dot(query.reshape(group, width)[:, mine], gq[:, cut], TN)
        value = value + dot(g_ref[:, mine], qp[:, cut], TN)
        value = value.reshape(wide, height, half)
        h_val[:, :, cut] = value
        h_ref[:, :, cut] = value.astype(BF16)

    def h_value(j, d):
        return h_val[net.owner(j, d)]

    def h_at(j, d):
        return h_ref.at[net.owner(j, d)]

    head_sum = Scatter(net, h_value, h_at, h_bufs[3:], half)
    head_sum.first(order)

    def h_block(j, e):
        return h_all.at[n, net.owner(j, e)]

    heads = Gather(net, h_block)
    sib = net.sems(wide * narrow)

    def share(j, e):
        for d in range(1, narrow):
            ref = h_block(j, e)
            net.send(ref, ref, sib + (j * depth + e) * narrow + d, net.sibling(d))

    row_grads(order[1])
    row_grads(order[2])
    rows_sum.second(order[0])
    for d in order:
        head_sum.second(d)
    rows_sum.first(order[1])
    rows_sum.first(order[2])
    mate_sem = net.sems(1)
    net.send(gq.at[queries_of(across), :], gq_mate.at[0], mate_sem, net.px)
    for i in range(3, depth):
        row_grads(order[i])
    for d in order:
        head_sum.third(d)
    for i in range(3, depth):
        rows_sum.first(order[i])
    total = head_sum.last()
    h_all[n, net.w] = total.astype(BF16)
    heads.start()
    share(0, 0)
    for i in range(1, depth):
        rows_sum.second(order[i])
    net.arrive(gq_mate.at[0], mate_sem)
    grad = gq[queries_of(me), :].astype(F32) + gq_mate[0].astype(F32)
    d_queries[...] = dot(grad.astype(BF16), head[...], NT)
    for e in range(1, depth):
        heads.column(e)
        share(0, e)
    for e in range(depth - 1):
        for j in (1, 2, 3):
            heads.plane(j, e)
            share(j, e)
    for j in (1, 2, 3):
        heads.plane(j, depth - 1)
        share(j, depth - 1)
    d_table[...] = rows_sum.last()
    for d in range(1, narrow):
        other = lax.rem(n - d + narrow, narrow)
        for j in range(4):
            for e in range(depth):
                ref = h_all.at[other, net.owner(j, e)]
                net.arrive(ref, sib + (j * depth + e) * narrow + d)
    d_head[...] = h_all[...]
    net.drain()


def finish(d_queries, d_table, d_head, out_queries, out_table, out_head, wide_head, sem):
    chunks, rows, _ = wide_head.shape
    copies = [
        pltpu.make_async_copy(d_queries, out_queries, sem.at[0]),
        pltpu.make_async_copy(d_table, out_table, sem.at[1]),
    ]
    for copy in copies:
        copy.start()
    for i in range(chunks):
        cut = pl.ds(i * rows, rows)
        wide_head[i] = d_head[cut, :].astype(F32)
        copies.append(
            pltpu.make_async_copy(wide_head.at[i], out_head.at[cut, :], sem.at[2 + i])
        )
        copies[-1].start()
    for copy in copies:
        copy.wait()


def per_device(queries, table, head, pos_ids, neg_ids, loss_weights):
    wide = lax.axis_size("wide")
    narrow = lax.axis_size("narrow")
    batch, width = queries.shape
    shard = table.shape[0]
    negatives = neg_ids.shape[1]
    part = shard // narrow
    depth = wide // 4
    span = depth * part
    team = 2 * narrow
    group = team * batch
    height = width // (narrow * wide)
    reduce_head = width % (8 * wide * narrow) == 0
    parts = (narrow, group) if reduce_head else (team, batch)
    scratch = [
        pltpu.VMEM((width, width), BF16),
        pltpu.VMEM((team, batch, width), BF16),
        pltpu.VMEM((team, negatives, batch), jnp.int32),
        pltpu.VMEM((team, 1, batch), jnp.int32),
        pltpu.VMEM((team, 1, batch), F32),
        pltpu.VMEM((2, depth, part, width), BF16),
        pltpu.VMEM((group, width), BF16),
        pltpu.VMEM((group, width), BF16),
        pltpu.VMEM((2, span, group), F32),
        pltpu.VMEM((2, span, group), F32),
        pltpu.VMEM((2, depth, part, group), BF16),
        pltpu.VMEM((team, 3, group), F32),
        pltpu.VMEM((group, width), F32),
        pltpu.VMEM(parts + (width,), BF16),
        pltpu.VMEM((narrow, group, width) if reduce_head else (1, 8, width), BF16),
        pltpu.VMEM((group, width), BF16),
        pltpu.VMEM((group, width), BF16),
        pltpu.VMEM((1 if reduce_head else team, batch, width), BF16),
        pltpu.VMEM((depth, 2, part, width), F32),
        pltpu.VMEM((depth, 2, part, width), BF16),
        pltpu.VMEM((depth, part, width), BF16),
        pltpu.VMEM((max(depth - 1, 1), part, width), BF16),
        pltpu.VMEM((max(depth - 1, 1), part, width), BF16),
    ]
    if reduce_head:
        scratch.append(pltpu.VMEM((wide, height, width), F32))
        scratch.append(pltpu.VMEM((wide, height, width), BF16))
        scratch.append(pltpu.VMEM((narrow, wide, height, width), BF16))
        scratch += scatter_bufs(depth, height, width)
        head_shape = jax.ShapeDtypeStruct((narrow, wide, height, width), BF16)
    else:
        head_shape = jax.ShapeDtypeStruct((width, width), F32)
    sems = 20 * depth + 3 + wide * narrow + 6 * team + 2 * narrow + 1
    sems = [
        pltpu.SemaphoreType.DMA((sems,)),
        pltpu.SemaphoreType.DMA((sems,)),
        pltpu.SemaphoreType.DMA((6,)),
    ]
    held = sum(math.prod(s.shape) * jnp.dtype(s.dtype).itemsize for s in scratch)
    limit = min(held + (16 << 20), 60 * 1024 * 1024)
    vmem = pl.BlockSpec(memory_space=pltpu.VMEM)
    hbm = pl.BlockSpec(memory_space=pltpu.HBM)
    shapes = (
        jax.ShapeDtypeStruct((batch, width), F32),
        jax.ShapeDtypeStruct((part, width), F32),
    )
    args = (queries, table, head, neg_ids.T, pos_ids[None, :], loss_weights[None, :])
    outs = pl.pallas_call(
        functools.partial(kernel, wide, narrow, reduce_head),
        out_shape=shapes + (head_shape,),
        in_specs=[hbm] * 6,
        out_specs=(vmem,) * 3,
        scratch_shapes=sems + scratch,
        compiler_params=pltpu.CompilerParams(
            collective_id=0, has_side_effects=True, vmem_limit_bytes=limit
        ),
    )(*[pltpu.with_memory_space_constraint(v, pltpu.HBM) for v in args])
    if not reduce_head:
        d_queries, d_table, d_head = outs
        return d_queries, d_table, lax.psum(d_head, BOTH)
    chunks = 4
    rows = width // chunks
    d_queries, d_table, d_head = outs
    return pl.pallas_call(
        finish,
        out_shape=shapes + (jax.ShapeDtypeStruct((width, width), F32),),
        in_specs=[vmem] * 3,
        out_specs=(hbm,) * 3,
        scratch_shapes=[
            pltpu.VMEM((chunks, rows, width), F32),
            pltpu.SemaphoreType.DMA((2 + chunks,)),
        ],
        compiler_params=pltpu.CompilerParams(vmem_limit_bytes=16000 * 1024),
    )(d_queries, d_table, d_head.reshape(width, width))


def solution(mesh):
    placed = (
        P(BOTH, None),
        P("wide", None),
        P(),
        P(BOTH),
        P(BOTH, None),
        P(BOTH),
    )
    return jax.shard_map(
        per_device,
        mesh=mesh,
        in_specs=placed,
        out_specs=(P(BOTH, None), P(BOTH, None), P()),
        check_vma=False,
    )
```
